32 devices in a mesh: gx: 4 (over y, x), gy: 4 (over z), gz: 2 (over core).
Axes of the slice: x: 2, y: 2, z: 4, core: 2. Of those that a mesh axis runs over, the one named last changes fastest.
Arguments:
- functions: bfloat16 [2560, 8, 4096], P(('gx', 'gy', 'gz')), may hold values from -6 to 6
- responses: bfloat16 [2560, 8, 4096], P(('gx', 'gy', 'gz')), may hold values from -6 to 6
- box_domain: int32 [2560, 1], P(('gx', 'gy', 'gz')), may hold values from 0 to 31, as said below
- pair_index: int32 [2, 2560, 24], P(None, ('gx', 'gy', 'gz')), may hold values from 0 to 7
- pair_weight: float32 [2560, 24], P(('gx', 'gy', 'gz')), may hold values from -6 to 6
- kernel_xc: float32 [32, 8192], P(('gx', 'gy', 'gz')), may hold values from 0.25 to 2
Outputs:
- applied: bfloat16 [2560, 8, 4096], P(('gx', 'gy', 'gz'))
- potential: bfloat16 [32, 8192], P(('gx', 'gy', 'gz'))
The draws below stay inside these ranges and needn't reach their ends.
Inputs may be any that keep to these rules, and one draw needn't show every extreme that they name: `box_domain`: boxes are held near their grid in y and z: a box of the device with mesh coordinates (ix, iy, iz) names domain ((ix + dx) mod 4, (iy + dy) mod 4, (iz + dz) mod 2) with dx in -2, -1, 0, dy in -1, 0 and dz in -1, 0, 1, and every device's boxes use all eighteen such offsets.
All inputs are finite; a program needn't handle non-finite values.
Results may differ from the reference program's by a relative error of at most 0.017.
Values may be sent and summed in bfloat16 or wider, within the bound.
A program may use at most 128 MiB of HBM per device.

```python
import math
import jax
import jax.numpy as jnp
from jax import lax

CB = 64
FB = 128
NFUN = 8
PAIRS = 24
BOX_DEV = 80
BOXES = 2560
N_GX = 4
N_GY = 4
N_GZ = 2
DEVICES = 32


def draw_box_domain(key, part):
    rows = jnp.arange(BOXES, dtype=jnp.int32)
    owner = rows // BOX_DEV
    within = rows % BOX_DEV
    key_codes = jax.random.fold_in(key, 11)
    key_shift = jax.random.fold_in(key, 23)
    codes = jax.random.randint(key_codes, (BOXES,), 0, 18, dtype=jnp.int32)
    shifts = jax.random.randint(key_shift, (DEVICES,), 0, 18, dtype=jnp.int32)
    first = (within + shifts[owner]) % 18
    codes = jnp.where(within < 18, first, codes)
    delta_x = codes // 6 - 2
    delta_y = codes // 3 % 2 - 1
    delta_z = codes % 3 - 1
    own_x = owner // (N_GY * N_GZ)
    own_y = owner // N_GZ % N_GY
    own_z = owner % N_GZ
    domain = ((own_x + delta_x) % N_GX * N_GY + (own_y + delta_y) % N_GY) * N_GZ + (own_z + delta_z) % N_GZ
    return domain[:, None].astype(jnp.int32)


def set_ends(values, own_key, low, largest):
    longest = values.shape.index(max(values.shape))
    spots = []
    for shift in (0, 1):
        where = [jax.random.randint(jax.random.fold_in(own_key, axis), (), 0, length) for axis, length in enumerate(values.shape)]
        where[longest] = (where[longest] + shift) % values.shape[longest]
        spots.append(tuple(where))
    return values.at[spots[0]].set(low).at[spots[1]].set(largest)


def level_of(stream_key, shape, cuts, smallest, high):
    factor_of, own = 1.0, jax.random.fold_in(stream_key, 6)
    for axis_at, parts in cuts:
        draws = jnp.exp(jax.random.uniform(jax.random.fold_in(own, axis_at), (parts,), jnp.float32, smallest / len(cuts), high / len(cuts)))
        factor_of = factor_of * jnp.repeat(draws, shape[axis_at] // parts).reshape([-1 if axis == axis_at else 1 for axis in range(len(shape))])
    return factor_of


def bell_draw(stream_key, dims, deviation, limit, pieces=(), held_as=jnp.bfloat16):
    loudness = level_of(stream_key, dims, pieces, -0.22, 0.18) if pieces else 1.0
    values = jax.random.normal(stream_key, dims, jnp.float32) * deviation * loudness
    return jnp.minimum(jnp.maximum(values, -limit), limit).astype(held_as)


def setup_inputs(seed: int = 0) -> dict:
    key_of = jax.random.split(jax.random.key(seed), 7)
    return {
        "functions": bell_draw(key_of[0], (BOXES, NFUN, CB * CB), 1.0, 6.0, ((0, 32),)),
        "responses": bell_draw(key_of[1], (BOXES, NFUN, CB * CB), 1.0, 6.0, ((0, 32),)),
        "box_domain": draw_box_domain(jax.random.fold_in(key_of[6], 71), 0),
        "pair_index": set_ends(jax.random.randint(key_of[3], (2, BOXES, PAIRS), 0, NFUN), jax.random.fold_in(key_of[3], 1), 0, NFUN - 1).astype(jnp.int32),
        "pair_weight": bell_draw(key_of[4], (BOXES, PAIRS), 0.4, 6.0, ((0, 32),), jnp.float32),
        "kernel_xc": jnp.clip(jnp.exp(math.log(2.0) - 2.0794415 * jax.random.uniform(key_of[5], (DEVICES, CB * FB), jnp.float32) ** level_of(key_of[5], (DEVICES, CB * FB), ((0, 32),), -0.2, 0.2)), 0.25, 2.0),
    }


HIGH = lax.Precision.HIGHEST


def interp_table(coarse):
    fine_len = 2 * coarse
    fine_pos = jnp.arange(fine_len, dtype=jnp.float32)[:, None]
    coarse_pos = jnp.arange(coarse, dtype=jnp.float32)[None, :]
    frequency = jnp.arange(1, coarse // 2, dtype=jnp.float32)[:, None, None]
    phases = 2.0 * jnp.pi * frequency * (fine_pos / fine_len - coarse_pos / coarse)
    summed = 1.0 + 2.0 * jnp.sum(jnp.cos(phases), axis=0) + jnp.cos(jnp.pi * coarse_pos) * jnp.cos(jnp.pi * fine_pos * coarse / fine_len)
    return (summed / coarse).astype(jnp.bfloat16)


def half_targets(domains, size_x, size_y, size_z):
    index_x = domains // (size_y * size_z)
    index_y = (domains // size_z) % size_y
    index_z = domains % size_z
    shift_x = jnp.array([0, 1], dtype=jnp.int32)
    return ((((index_x[:, None] + shift_x[None, :]) % size_x) * size_y + index_y[:, None]) * size_z + index_z[:, None]).astype(jnp.int32)


def interpolate(planes, table_full):
    box_count, fun_count = planes.shape[0], planes.shape[1]
    shaped = planes.reshape(box_count, fun_count, CB, CB).astype(jnp.float32)
    table = table_full.astype(jnp.float32)
    stretched = jnp.einsum('bfxy,Xx->bfyX', shaped, table, precision=HIGH).astype(jnp.bfloat16)
    return jnp.einsum('bfyX,Yy->bfXY', stretched.astype(jnp.float32), table, precision=HIGH).astype(jnp.bfloat16)


def block_density(func_blk, resp_blk, pidx_blk, weight_blk, table_full):
    fine_f = interpolate(func_blk, table_full)
    fine_r = interpolate(resp_blk, table_full)
    levels = jnp.arange(NFUN, dtype=jnp.int32)
    first_hot = (pidx_blk[0][..., None] == levels).astype(jnp.float32)
    second_hot = (pidx_blk[1][..., None] == levels).astype(jnp.float32)
    kernel_pairs = jnp.einsum('bp,bpf,bpg->bfg', weight_blk, first_hot, second_hot, precision=HIGH).astype(jnp.bfloat16)
    mixed_resp = jnp.einsum('bfg,bgXY->bfXY', kernel_pairs.astype(jnp.float32), fine_r.astype(jnp.float32), precision=HIGH)
    density = jnp.sum(fine_f.astype(jnp.float32) * mixed_resp, axis=1)
    return density.reshape(density.shape[0], 2, CB * FB)


def block_apply(fine_f, box_pot, table_half):
    table = table_half.astype(jnp.float32)
    weighted = (box_pot[:, None].astype(jnp.float32) * fine_f.astype(jnp.float32)).astype(jnp.bfloat16)
    colwise = jnp.einsum('bfXY,Xx->bfYx', weighted.astype(jnp.float32), table, precision=HIGH).astype(jnp.bfloat16)
    result = jnp.einsum('bfYx,Yy->bfxy', colwise.astype(jnp.float32), table, precision=HIGH).astype(jnp.bfloat16)
    return result.reshape(result.shape[0], result.shape[1], CB * CB)


def reference(functions, responses, box_domain, pair_index, pair_weight, kernel_xc):
    table_full = interp_table(CB)
    table_half = table_full * 0.5
    blocks = BOXES // 16
    targets = half_targets(box_domain[:, 0], N_GX, N_GY, N_GZ)

    def blocked(array):
        return array.reshape((blocks, 16) + array.shape[1:])

    pidx_blocks = pair_index.reshape(2, blocks, 16, PAIRS).transpose(1, 0, 2, 3)

    def deposit_step(accumulated, inputs):
        func_blk, resp_blk, pidx_blk, weight_blk, target_blk = inputs
        halves = block_density(func_blk, resp_blk, pidx_blk, weight_blk, table_full)
        return accumulated.at[target_blk.reshape(-1)].add(halves.reshape(-1, CB * FB)), None

    start = jnp.zeros((DEVICES, CB * FB), jnp.float32)
    accumulated, _ = lax.scan(deposit_step, start, (blocked(functions), blocked(responses), pidx_blocks, blocked(pair_weight), blocked(targets)))
    potential = (kernel_xc * accumulated).astype(jnp.bfloat16)

    def apply_step(inputs):
        func_blk, target_blk = inputs
        fine_f = interpolate(func_blk, table_full)
        box_pot = potential[target_blk].reshape(target_blk.shape[0], FB, FB)
        return block_apply(fine_f, box_pot, table_half)

    applied = lax.map(apply_step, (blocked(functions), blocked(targets))).reshape(BOXES, NFUN, CB * CB)
    return applied, potential
```

```python
import functools
import math

import jax
import jax.numpy as jnp
import numpy as np
from jax import lax
from jax.experimental import pallas as pl
from jax.experimental.pallas import tpu as pltpu
from jax.sharding import PartitionSpec as P

MESH = pl.DeviceIdType.MESH
F32 = jnp.float32
BF16 = jnp.bfloat16
STEP_BOXES = 16


def interp_table(coarse):
    fine = 2 * coarse
    m = np.arange(fine, dtype=np.float64)[:, None]
    n = np.arange(coarse, dtype=np.float64)[None, :]
    k = np.arange(1, coarse // 2, dtype=np.float64)[:, None, None]
    total = 1.0 + 2.0 * np.sum(np.cos(2.0 * np.pi * k * (m / fine - n / coarse)), axis=0)
    total = total + np.cos(np.pi * n) * np.cos(np.pi * m * coarse / fine)
    return total / coarse


def tables(coarse):
    odd = interp_table(coarse)[1::2]
    order = np.concatenate([np.arange(0, coarse, 2), np.arange(1, coarse, 2)])
    along_x = odd[order][:, order]
    quad = np.eye(4)
    rows = np.array(
        [4 * jj + 2 * p + xp for xp in range(2) for p in range(2) for jj in range(coarse // 4)]
    )
    cols = np.array([2 * y + yp for yp in range(2) for y in range(coarse)])
    row_pick = np.zeros((coarse, coarse))
    row_pick[np.arange(coarse), rows] = 1.0
    col_pick = np.zeros((2 * coarse, 2 * coarse))
    col_pick[cols, np.arange(2 * coarse)] = 1.0

    def low(array):
        return jnp.asarray(np.ascontiguousarray(array), F32).astype(BF16)

    return {
        "ax": low(along_x),
        "axt": low(along_x.T),
        "yup": low(np.kron(quad, odd.T)),
        "ydown": low(np.kron(quad, odd)),
        "row": low(row_pick),
        "rowt": low(row_pick.T),
        "col": low(col_pick),
        "colt": low(col_pick.T),
    }


def dot(a, b):
    return jnp.dot(a, b, preferred_element_type=F32)


def density_kernel(
    coarse, steps, slots, bd, func, resp, ax, yup, fe, fo, part, rm, sf, sr, me, mo, acc
):
    step = pl.program_id(0)
    half = coarse // 2
    quarter = coarse // 4
    lanes = 2 * coarse
    left = lax.broadcasted_iota(jnp.int32, (half, lanes), 1) < coarse
    left_all = lax.broadcasted_iota(jnp.int32, (lanes, lanes), 1) < coarse

    @pl.when(step == 0)
    def _():
        acc[...] = jnp.zeros_like(acc)

    width = 512
    for c in range(0, coarse * coarse, width):
        rm[:, c : c + width] = dot(bd[...], resp[:, c : c + width])

    def pair(i, carry):
        r0 = pl.multiple_of(i * 16, 16)
        g0 = i * 4
        for src, s, even, odd, at in ((func, sf, fe, fo, g0), (rm, sr, me, mo, 0)):
            for j in range(half):
                s[pl.ds(j, 16, stride=half), :] = src[
                    pl.ds(r0, 16), j * lanes : (j + 1) * lanes
                ].astype(F32)
            for g in range(4):
                t = [s[(4 * g + k) * half : (4 * g + k + 1) * half, :] for k in range(4)]
                evens, odds = [], []
                for k in (0, 2):
                    evens.append(jnp.where(left, t[k], pltpu.roll(t[k + 1], coarse, 1)))
                    odds.append(jnp.where(left, pltpu.roll(t[k], coarse, 1), t[k + 1]))
                x = jnp.concatenate(
                    [jnp.concatenate(evens, axis=1), jnp.concatenate(odds, axis=1)], axis=0
                ).astype(BF16)
                up = dot(ax[...], x).astype(BF16)
                even[at + g, 0:coarse, :] = x
                even[at + g, coarse:lanes, :] = up
                both = jnp.concatenate([x, up], axis=0)
                odd[at + g, :, :] = dot(both, yup[...]).astype(BF16)
        for b in range(2):
            sums = []
            for left_src, right_src in ((fe, me), (fo, mo)):
                total = None
                for g in (2 * b, 2 * b + 1):
                    prod = left_src[g0 + g].astype(F32) * right_src[g].astype(F32)
                    prod = prod[:, :lanes] + prod[:, lanes:]
                    total = prod if total is None else total + prod
                sums.append(total + pltpu.roll(total, coarse, 1))
            d = jnp.where(left_all, sums[0], sums[1])
            at = (step * STEP_BOXES + 2 * i + b) * 2
            for q in range(2):
                slot = slots[at + q]
                for c in range(4):
                    acc[slot, c * quarter : (c + 1) * quarter, :] += d[
                        c * half + q * quarter : c * half + (q + 1) * quarter, :
                    ]
        return carry

    lax.fori_loop(0, STEP_BOXES // 2, pair, 0)

    @pl.when(step == steps - 1)
    def _():
        part[...] = acc[...].astype(BF16)


def exchange_kernel(
    sizes, shifts, own, part, kxc, row, rowt, col, colt, ve, vo, out, got, pot, back, s1, r1, s2, r2
):
    coarse = kxc.shape[0]
    me = [lax.axis_index(name) for name in ("gx", "gy", "gz")]

    def device(shift, sign):
        return tuple(
            lax.rem(me[a] + (sign * shift[a]) % sizes[a], sizes[a]) for a in range(3)
        )

    others = [k for k in range(len(shifts)) if k != own]
    barrier = pltpu.get_barrier_semaphore()
    for k in others:
        pl.semaphore_signal(
            barrier, inc=1, device_id=device(shifts[k], -1), device_id_type=MESH
        )
    pl.semaphore_wait(barrier, len(others))
    first, second = {}, {}
    for k in others:
        first[k] = pltpu.make_async_remote_copy(
            src_ref=part.at[k],
            dst_ref=got.at[k],
            send_sem=s1.at[k],
            recv_sem=r1.at[k],
            device_id=device(shifts[k], 1),
            device_id_type=MESH,
        )
        first[k].start()
    high = lax.Precision.HIGHEST
    by_col = jnp.dot(kxc[...], col[...].astype(F32), precision=high)
    scale = jnp.dot(row[...].astype(F32), by_col, precision=high)
    total = part[own].astype(F32)
    for k in others:
        first[k].wait_recv()
        total = total + got[k].astype(F32)
    value = (scale * total).astype(BF16)
    pot[...] = value
    for k in others:
        second[k] = pltpu.make_async_remote_copy(
            src_ref=pot,
            dst_ref=back.at[k],
            send_sem=s2.at[k],
            recv_sem=r2.at[k],
            device_id=device(shifts[k], -1),
            device_id_type=MESH,
        )
        second[k].start()
    by_col = dot(value, colt[...]).astype(BF16)
    out[...] = dot(rowt[...], by_col).astype(BF16)
    left = lax.broadcasted_iota(jnp.int32, value.shape, 1) < coarse

    def spread(k, block):
        block = block.astype(F32)
        turned = pltpu.roll(block, coarse, 1)
        ve[k] = jnp.where(left, block, turned).astype(BF16)
        vo[k] = jnp.where(left, turned, block).astype(BF16)

    spread(own, value)
    for k in others:
        second[k].wait_recv()
        spread(k, back[k])
    for k in others:
        first[k].wait_send()
        second[k].wait_send()


def apply_kernel(coarse, slots, fe, fo, ve, vo, axt, ydown, out, s):
    step = pl.program_id(0)
    half = coarse // 2
    quarter = coarse // 4
    lanes = 2 * coarse
    left = lax.broadcasted_iota(jnp.int32, (half, lanes), 1) < coarse

    def pair(i, carry):
        r0 = pl.multiple_of(i * 16, 16)
        g0 = i * 4
        for b in range(2):
            at = (step * STEP_BOXES + 2 * i + b) * 2
            pieces = []
            for v in (ve, vo):
                rows = []
                for c in range(4):
                    for q in range(2):
                        rows.append(v[slots[at + q], c * quarter : (c + 1) * quarter, :])
                plane = jnp.concatenate(rows, axis=0)
                pieces.append(jnp.concatenate([plane, plane], axis=1))
            for g in (2 * b, 2 * b + 1):
                we = fe[g0 + g] * pieces[0]
                wo = fo[g0 + g] * pieces[1]
                z = we.astype(F32) + dot(wo, ydown[...])
                down = dot(axt[...], z[coarse:].astype(BF16))
                res = (z[:coarse] + down) * 0.25
                for k in (0, 2):
                    e = res[:half, k * coarse : (k + 2) * coarse]
                    o = res[half:, k * coarse : (k + 2) * coarse]
                    base = (4 * g + k) * half
                    s[base : base + half, :] = jnp.where(left, e, pltpu.roll(o, coarse, 1))
                    s[base + half : base + 2 * half, :] = jnp.where(
                        left, pltpu.roll(e, coarse, 1), o
                    )
        for j in range(half):
            out[pl.ds(r0, 16), j * lanes : (j + 1) * lanes] = s[
                pl.ds(j, 16, stride=half), :
            ].astype(BF16)
        return carry

    lax.fori_loop(0, STEP_BOXES // 2, pair, 0)


def on_device(sizes, functions, responses, box_domain, pair_index, pair_weight, kernel_xc):
    boxes, funs, cells = functions.shape
    coarse = math.isqrt(cells)
    lanes = 2 * coarse
    size_x, size_y, size_z = sizes
    near = (min(4, size_x), min(2, size_y), min(3, size_z))
    shifts = [
        (kx - 2, ky - 1, kz - 1)
        for kx in range(near[0])
        for ky in range(near[1])
        for kz in range(near[2])
    ]
    own = [k for k, sh in enumerate(shifts) if all(d % n == 0 for d, n in zip(sh, sizes))][0]
    count = len(shifts)
    t = tables(coarse)

    domain = box_domain[:, 0]
    tx = domain // (size_y * size_z)
    ty = domain // size_z % size_y
    tz = domain % size_z
    kx = (tx[:, None] + jnp.arange(2, dtype=jnp.int32) - lax.axis_index("gx") + 2) % size_x
    ky = (ty - lax.axis_index("gy") + 1) % size_y
    kz = (tz - lax.axis_index("gz") + 1) % size_z
    slots = (kx * near[1] + ky[:, None]) * near[2] + kz[:, None]
    slots = jnp.clip(slots, 0, count - 1).astype(jnp.int32).reshape(-1)

    rows = STEP_BOXES * funs
    first, second = pair_index[0], pair_index[1]
    f_of = jnp.arange(funs, dtype=jnp.int32)
    lane = jnp.arange(rows, dtype=jnp.int32)
    weight_f = jnp.where(first[:, None, :] == f_of[None, :, None], pair_weight[:, None, :], 0.0)
    same = second[:, None, :, None] == (lane % funs)[None, None, None, :]
    mixed = jnp.sum(jnp.where(same, weight_f[..., None], 0.0), axis=2)
    here = (jnp.arange(boxes, dtype=jnp.int32) % STEP_BOXES)[:, None] == (lane // funs)[None, :]
    bd = jnp.where(here[:, None, :], mixed, 0.0).astype(BF16).reshape(boxes * funs, rows)

    steps = boxes // STEP_BOXES
    groups = STEP_BOXES * funs // 4

    def whole(shape):
        return pl.BlockSpec(shape, lambda i, *_: (0,) * len(shape))

    fe, fo, part = pl.pallas_call(
        functools.partial(density_kernel, coarse, steps),
        grid_spec=pltpu.PrefetchScalarGridSpec(
            num_scalar_prefetch=1,
            grid=(steps,),
            in_specs=[
                pl.BlockSpec((rows, rows), lambda i, *_: (i, 0)),
                pl.BlockSpec((rows, cells), lambda i, *_: (i, 0)),
                pl.BlockSpec((rows, cells), lambda i, *_: (i, 0)),
                whole((coarse, coarse)),
                whole((4 * coarse, 4 * coarse)),
            ],
            out_specs=[
                pl.BlockSpec((groups, lanes, 4 * coarse), lambda i, *_: (i, 0, 0)),
                pl.BlockSpec((groups, lanes, 4 * coarse), lambda i, *_: (i, 0, 0)),
                whole((count, coarse, lanes)),
            ],
            scratch_shapes=[
                pltpu.VMEM((rows, cells), F32),
                pltpu.VMEM((16 * coarse // 2, lanes), F32),
                pltpu.VMEM((16 * coarse // 2, lanes), F32),
                pltpu.VMEM((4, lanes, 4 * coarse), BF16),
                pltpu.VMEM((4, lanes, 4 * coarse), BF16),
                pltpu.VMEM((count, coarse, lanes), F32),
            ],
        ),
        out_shape=[
            jax.ShapeDtypeStruct((steps * groups, lanes, 4 * coarse), BF16),
            jax.ShapeDtypeStruct((steps * groups, lanes, 4 * coarse), BF16),
            jax.ShapeDtypeStruct((count, coarse, lanes), BF16),
        ],
        name="density",
    )(
        slots,
        bd,
        functions.reshape(boxes * funs, cells),
        responses.reshape(boxes * funs, cells),
        t["ax"],
        t["yup"],
    )

    vm = pl.BlockSpec(memory_space=pltpu.VMEM)
    block = (count, coarse, lanes)
    ve, vo, potential = pl.pallas_call(
        functools.partial(exchange_kernel, sizes, shifts, own),
        in_specs=[vm] * 6,
        out_specs=[vm] * 3,
        out_shape=[
            jax.ShapeDtypeStruct(block, BF16),
            jax.ShapeDtypeStruct(block, BF16),
            jax.ShapeDtypeStruct((coarse, lanes), BF16),
        ],
        scratch_shapes=[
            pltpu.VMEM(block, BF16),
            pltpu.VMEM((coarse, lanes), BF16),
            pltpu.VMEM(block, BF16),
        ]
        + [pltpu.SemaphoreType.DMA((count,))] * 4,
        compiler_params=pltpu.CompilerParams(collective_id=0, has_side_effects=True),
        name="exchange",
    )(part, kernel_xc.reshape(coarse, lanes), t["row"], t["rowt"], t["col"], t["colt"])

    applied = pl.pallas_call(
        functools.partial(apply_kernel, coarse),
        grid_spec=pltpu.PrefetchScalarGridSpec(
            num_scalar_prefetch=1,
            grid=(steps,),
            in_specs=[
                pl.BlockSpec((groups, lanes, 4 * coarse), lambda i, *_: (i, 0, 0)),
                pl.BlockSpec((groups, lanes, 4 * coarse), lambda i, *_: (i, 0, 0)),
                whole(block),
                whole(block),
                whole((coarse, coarse)),
                whole((4 * coarse, 4 * coarse)),
            ],
            out_specs=pl.BlockSpec((rows, cells), lambda i, *_: (i, 0)),
            scratch_shapes=[pltpu.VMEM((16 * coarse // 2, lanes), F32)],
        ),
        out_shape=jax.ShapeDtypeStruct((boxes * funs, cells), BF16),
        name="apply",
    )(slots, fe, fo, ve, vo, t["axt"], t["ydown"])
    return applied.reshape(boxes, funs, cells), potential.reshape(1, coarse * lanes)


def solution(mesh):
    sizes = tuple(mesh.shape[name] for name in ("gx", "gy", "gz"))
    over = ("gx", "gy", "gz")
    in_specs = (
        P(over, None, None),
        P(over, None, None),
        P(over, None),
        P(None, over, None),
        P(over, None),
        P(over, None),
    )
    out_specs = (P(over, None, None), P(over, None))
    return jax.shard_map(
        functools.partial(on_device, sizes),
        mesh=mesh,
        in_specs=in_specs,
        out_specs=out_specs,
        check_vma=False,
    )
```

```python
import functools
import math

import jax
import jax.numpy as jnp
import numpy as np
from jax import lax
from jax.experimental import pallas as pl
from jax.experimental.pallas import tpu as pltpu
from jax.sharding import PartitionSpec as P

MESH = pl.DeviceIdType.MESH
F32 = jnp.float32
BF16 = jnp.bfloat16
STEP_BOXES = 16


def interp_table(coarse):
    fine = 2 * coarse
    m = np.arange(fine, dtype=np.float64)[:, None]
    n = np.arange(coarse, dtype=np.float64)[None, :]
    k = np.arange(1, coarse // 2, dtype=np.float64)[:, None, None]
    total = 1.0 + 2.0 * np.sum(np.cos(2.0 * np.pi * k * (m / fine - n / coarse)), axis=0)
    total = total + np.cos(np.pi * n) * np.cos(np.pi * m * coarse / fine)
    return total / coarse


def tables(coarse):
    odd = interp_table(coarse)[1::2]
    order = np.concatenate([np.arange(0, coarse, 2), np.arange(1, coarse, 2)])
    along_x = odd[order][:, order]
    quad = np.eye(4)
    rows = np.array(
        [4 * jj + 2 * p + xp for xp in range(2) for p in range(2) for jj in range(coarse // 4)]
    )
    cols = np.array([2 * y + yp for yp in range(2) for y in range(coarse)])
    row_pick = np.zeros((coarse, coarse))
    row_pick[np.arange(coarse), rows] = 1.0
    col_pick = np.zeros((2 * coarse, 2 * coarse))
    col_pick[cols, np.arange(2 * coarse)] = 1.0

    tile = 16
    turn = np.zeros((tile * tile, tile * tile))
    for r in range(tile):
        for jj in range(tile):
            turn[r * tile + jj, jj * tile + r] = 1.0

    def low(array):
        return jnp.asarray(np.ascontiguousarray(array), F32).astype(BF16)

    return {
        "ax": low(along_x),
        "axt": low(along_x.T),
        "yup": low(np.kron(quad, odd.T)),
        "ydown": low(np.kron(quad, odd)),
        "turn": low(turn),
        "row": low(row_pick),
        "rowt": low(row_pick.T),
        "col": low(col_pick),
        "colt": low(col_pick.T),
    }


def dot(a, b):
    return jnp.dot(a, b, preferred_element_type=F32)


def stacked(src, r0, lanes):
    tiles = [src[pl.ds(r0, 16), j * lanes : (j + 1) * lanes] for j in range(32)]
    return jnp.concatenate(
        [jnp.concatenate(tiles[:16], axis=0), jnp.concatenate(tiles[16:], axis=0)], axis=1
    )


def density_kernel(
    coarse, steps, slots, bd, func, resp, ax, yup, turn, fe, fo, part, rm, me, mo, acc
):
    step = pl.program_id(0)
    half = coarse // 2
    quarter = coarse // 4
    lanes = 2 * coarse
    left = lax.broadcasted_iota(jnp.int32, (half, lanes), 1) < coarse
    left_all = lax.broadcasted_iota(jnp.int32, (lanes, lanes), 1) < coarse

    @pl.when(step == 0)
    def _():
        acc[...] = jnp.zeros_like(acc)

    width = 512
    for c in range(0, coarse * coarse, width):
        rm[:, c : c + width] = dot(bd[...], resp[:, c : c + width]).astype(BF16)

    def pair(i, carry):
        r0 = pl.multiple_of(i * 16, 16)
        g0 = i * 4
        for src, even, odd, at in ((func, fe, fo, g0), (rm, me, mo, 0)):
            t_all = dot(turn[...], stacked(src, r0, lanes))
            for g in range(4):
                t = []
                for k in range(4 * g, 4 * g + 4):
                    piece = t_all[16 * k : 16 * k + 16]
                    t.append(jnp.concatenate([piece[:, :lanes], piece[:, lanes:]], axis=0))
                evens, odds = [], []
                for k in (0, 2):
                    evens.append(jnp.where(left, t[k], pltpu.roll(t[k + 1], coarse, 1)))
                    odds.append(jnp.where(left, pltpu.roll(t[k], coarse, 1), t[k + 1]))
                x = jnp.concatenate(
                    [jnp.concatenate(evens, axis=1), jnp.concatenate(odds, axis=1)], axis=0
                ).astype(BF16)
                up = dot(ax[...], x).astype(BF16)
                even[at + g, 0:coarse, :] = x
                even[at + g, coarse:lanes, :] = up
                both = jnp.concatenate([x, up], axis=0)
                odd[at + g, :, :] = dot(both, yup[...]).astype(BF16)
        for b in range(2):
            sums = []
            for left_src, right_src in ((fe, me), (fo, mo)):
                total = None
                for g in (2 * b, 2 * b + 1):
                    prod = (left_src[g0 + g] * right_src[g]).astype(F32)
                    prod = prod[:, :lanes] + prod[:, lanes:]
                    total = prod if total is None else total + prod
                sums.append(total + pltpu.roll(total, coarse, 1))
            d = jnp.where(left_all, sums[0], sums[1])
            at = (step * STEP_BOXES + 2 * i + b) * 2
            for q in range(2):
                slot = slots[at + q]
                for c in range(4):
                    acc[slot, c * quarter : (c + 1) * quarter, :] += d[
                        c * half + q * quarter : c * half + (q + 1) * quarter, :
                    ]
        return carry

    lax.fori_loop(0, STEP_BOXES // 2, pair, 0)

    @pl.when(step == steps - 1)
    def _():
        part[...] = acc[...].astype(BF16)


def exchange_kernel(
    sizes, shifts, own, part, kxc, row, rowt, col, colt, ve, vo, out, got, pot, back, s1, r1, s2, r2
):
    coarse = kxc.shape[0]
    me = [lax.axis_index(name) for name in ("gx", "gy", "gz")]

    def device(shift, sign):
        return tuple(
            lax.rem(me[a] + (sign * shift[a]) % sizes[a], sizes[a]) for a in range(3)
        )

    others = [k for k in range(len(shifts)) if k != own]
    barrier = pltpu.get_barrier_semaphore()
    for k in others:
        pl.semaphore_signal(
            barrier, inc=1, device_id=device(shifts[k], -1), device_id_type=MESH
        )
    pl.semaphore_wait(barrier, len(others))
    first, second = {}, {}
    for k in others:
        first[k] = pltpu.make_async_remote_copy(
            src_ref=part.at[k],
            dst_ref=got.at[k],
            send_sem=s1.at[k],
            recv_sem=r1.at[k],
            device_id=device(shifts[k], 1),
            device_id_type=MESH,
        )
        first[k].start()
    high = lax.Precision.HIGHEST
    by_col = jnp.dot(kxc[...], col[...].astype(F32), precision=high)
    scale = jnp.dot(row[...].astype(F32), by_col, precision=high)
    total = part[own].astype(F32)
    for k in others:
        first[k].wait_recv()
        total = total + got[k].astype(F32)
    value = (scale * total).astype(BF16)
    pot[...] = value
    for k in others:
        second[k] = pltpu.make_async_remote_copy(
            src_ref=pot,
            dst_ref=back.at[k],
            send_sem=s2.at[k],
            recv_sem=r2.at[k],
            device_id=device(shifts[k], -1),
            device_id_type=MESH,
        )
        second[k].start()
    by_col = dot(value, colt[...]).astype(BF16)
    out[...] = dot(rowt[...], by_col).astype(BF16)
    left = lax.broadcasted_iota(jnp.int32, value.shape, 1) < coarse

    def spread(k, block):
        block = block.astype(F32)
        turned = pltpu.roll(block, coarse, 1)
        ve[k] = jnp.where(left, block, turned).astype(BF16)
        vo[k] = jnp.where(left, turned, block).astype(BF16)

    spread(own, value)
    for k in others:
        second[k].wait_recv()
        spread(k, back[k])
    for k in others:
        first[k].wait_send()
        second[k].wait_send()


def apply_kernel(coarse, slots, fe, fo, ve, vo, axt, ydown, back, out):
    step = pl.program_id(0)
    half = coarse // 2
    quarter = coarse // 4
    lanes = 2 * coarse
    left = lax.broadcasted_iota(jnp.int32, (half, lanes), 1) < coarse

    def pair(i, carry):
        r0 = pl.multiple_of(i * 16, 16)
        g0 = i * 4
        pieces_out = []
        for b in range(2):
            at = (step * STEP_BOXES + 2 * i + b) * 2
            pieces = []
            for v in (ve, vo):
                rows = []
                for c in range(4):
                    for q in range(2):
                        rows.append(v[slots[at + q], c * quarter : (c + 1) * quarter, :])
                plane = jnp.concatenate(rows, axis=0)
                pieces.append(jnp.concatenate([plane, plane], axis=1))
            for g in (2 * b, 2 * b + 1):
                we = fe[g0 + g] * pieces[0]
                wo = fo[g0 + g] * pieces[1]
                z = we.astype(F32) + dot(wo, ydown[...])
                down = dot(axt[...], z[coarse:].astype(BF16))
                res = (z[:coarse] + down) * 0.25
                for k in (0, 2):
                    e = res[:half, k * coarse : (k + 2) * coarse]
                    o = res[half:, k * coarse : (k + 2) * coarse]
                    first = jnp.where(left, e, pltpu.roll(o, coarse, 1)).astype(BF16)
                    second = jnp.where(left, pltpu.roll(e, coarse, 1), o).astype(BF16)
                    for block in (first, second):
                        pieces_out.append(jnp.concatenate([block[:16], block[16:]], axis=1))
        flat = dot(back[...], jnp.concatenate(pieces_out, axis=0)).astype(BF16)
        for j in range(half):
            jj, h = j % 16, j // 16
            out[pl.ds(r0, 16), j * lanes : (j + 1) * lanes] = flat[
                16 * jj : 16 * jj + 16, h * lanes : (h + 1) * lanes
            ]
        return carry

    lax.fori_loop(0, STEP_BOXES // 2, pair, 0)


def on_device(sizes, functions, responses, box_domain, pair_index, pair_weight, kernel_xc):
    boxes, funs, cells = functions.shape
    coarse = math.isqrt(cells)
    lanes = 2 * coarse
    size_x, size_y, size_z = sizes
    near = (min(4, size_x), min(2, size_y), min(3, size_z))
    shifts = [
        (kx - 2, ky - 1, kz - 1)
        for kx in range(near[0])
        for ky in range(near[1])
        for kz in range(near[2])
    ]
    own = [k for k, sh in enumerate(shifts) if all(d % n == 0 for d, n in zip(sh, sizes))][0]
    count = len(shifts)
    t = tables(coarse)

    domain = box_domain[:, 0]
    tx = domain // (size_y * size_z)
    ty = domain // size_z % size_y
    tz = domain % size_z
    kx = (tx[:, None] + jnp.arange(2, dtype=jnp.int32) - lax.axis_index("gx") + 2) % size_x
    ky = (ty - lax.axis_index("gy") + 1) % size_y
    kz = (tz - lax.axis_index("gz") + 1) % size_z
    slots = (kx * near[1] + ky[:, None]) * near[2] + kz[:, None]
    slots = jnp.clip(slots, 0, count - 1).astype(jnp.int32).reshape(-1)

    rows = STEP_BOXES * funs
    first, second = pair_index[0], pair_index[1]
    f_of = jnp.arange(funs, dtype=jnp.int32)
    lane = jnp.arange(rows, dtype=jnp.int32)
    weight_f = jnp.where(first[:, None, :] == f_of[None, :, None], pair_weight[:, None, :], 0.0)
    same = second[:, None, :, None] == (lane % funs)[None, None, None, :]
    mixed = jnp.sum(jnp.where(same, weight_f[..., None], 0.0), axis=2)
    here = (jnp.arange(boxes, dtype=jnp.int32) % STEP_BOXES)[:, None] == (lane // funs)[None, :]
    bd = jnp.where(here[:, None, :], mixed, 0.0).astype(BF16).reshape(boxes * funs, rows)

    steps = boxes // STEP_BOXES
    groups = STEP_BOXES * funs // 4

    def whole(shape):
        return pl.BlockSpec(shape, lambda i, *_: (0,) * len(shape))

    fe, fo, part = pl.pallas_call(
        functools.partial(density_kernel, coarse, steps),
        grid_spec=pltpu.PrefetchScalarGridSpec(
            num_scalar_prefetch=1,
            grid=(steps,),
            in_specs=[
                pl.BlockSpec((rows, rows), lambda i, *_: (i, 0)),
                pl.BlockSpec((rows, cells), lambda i, *_: (i, 0)),
                pl.BlockSpec((rows, cells), lambda i, *_: (i, 0)),
                whole((coarse, coarse)),
                whole((4 * coarse, 4 * coarse)),
                whole((256, 256)),
            ],
            out_specs=[
                pl.BlockSpec((groups, lanes, 4 * coarse), lambda i, *_: (i, 0, 0)),
                pl.BlockSpec((groups, lanes, 4 * coarse), lambda i, *_: (i, 0, 0)),
                whole((count, coarse, lanes)),
            ],
            scratch_shapes=[
                pltpu.VMEM((rows, cells), BF16),
                pltpu.VMEM((4, lanes, 4 * coarse), BF16),
                pltpu.VMEM((4, lanes, 4 * coarse), BF16),
                pltpu.VMEM((count, coarse, lanes), F32),
            ],
        ),
        out_shape=[
            jax.ShapeDtypeStruct((steps * groups, lanes, 4 * coarse), BF16),
            jax.ShapeDtypeStruct((steps * groups, lanes, 4 * coarse), BF16),
            jax.ShapeDtypeStruct((count, coarse, lanes), BF16),
        ],
        name="density",
    )(
        slots,
        bd,
        functions.reshape(boxes * funs, cells),
        responses.reshape(boxes * funs, cells),
        t["ax"],
        t["yup"],
        t["turn"],
    )

    vm = pl.BlockSpec(memory_space=pltpu.VMEM)
    block = (count, coarse, lanes)
    ve, vo, potential = pl.pallas_call(
        functools.partial(exchange_kernel, sizes, shifts, own),
        in_specs=[vm] * 6,
        out_specs=[vm] * 3,
        out_shape=[
            jax.ShapeDtypeStruct(block, BF16),
            jax.ShapeDtypeStruct(block, BF16),
            jax.ShapeDtypeStruct((coarse, lanes), BF16),
        ],
        scratch_shapes=[
            pltpu.VMEM(block, BF16),
            pltpu.VMEM((coarse, lanes), BF16),
            pltpu.VMEM(block, BF16),
        ]
        + [pltpu.SemaphoreType.DMA((count,))] * 4,
        compiler_params=pltpu.CompilerParams(collective_id=0, has_side_effects=True),
        name="exchange",
    )(part, kernel_xc.reshape(coarse, lanes), t["row"], t["rowt"], t["col"], t["colt"])

    applied = pl.pallas_call(
        functools.partial(apply_kernel, coarse),
        grid_spec=pltpu.PrefetchScalarGridSpec(
            num_scalar_prefetch=1,
            grid=(steps,),
            in_specs=[
                pl.BlockSpec((groups, lanes, 4 * coarse), lambda i, *_: (i, 0, 0)),
                pl.BlockSpec((groups, lanes, 4 * coarse), lambda i, *_: (i, 0, 0)),
                whole(block),
                whole(block),
                whole((coarse, coarse)),
                whole((4 * coarse, 4 * coarse)),
                whole((256, 256)),
            ],
            out_specs=pl.BlockSpec((rows, cells), lambda i, *_: (i, 0)),
        ),
        out_shape=jax.ShapeDtypeStruct((boxes * funs, cells), BF16),
        name="apply",
    )(slots, fe, fo, ve, vo, t["axt"], t["ydown"], t["turn"])
    return applied.reshape(boxes, funs, cells), potential.reshape(1, coarse * lanes)


def solution(mesh):
    sizes = tuple(mesh.shape[name] for name in ("gx", "gy", "gz"))
    over = ("gx", "gy", "gz")
    in_specs = (
        P(over, None, None),
        P(over, None, None),
        P(over, None),
        P(None, over, None),
        P(over, None),
        P(over, None),
    )
    out_specs = (P(over, None, None), P(over, None))
    return jax.shard_map(
        functools.partial(on_device, sizes),
        mesh=mesh,
        in_specs=in_specs,
        out_specs=out_specs,
        check_vma=False,
    )
```

```python
import functools
import math

import jax
import jax.numpy as jnp
import numpy as np
from jax import lax
from jax.experimental import pallas as pl
from jax.experimental.pallas import tpu as pltpu
from jax.sharding import PartitionSpec as P

MESH = pl.DeviceIdType.MESH
F32 = jnp.float32
BF16 = jnp.bfloat16
STEP_BOXES = 16


def interp_table(coarse):
    fine = 2 * coarse
    m = np.arange(fine, dtype=np.float64)[:, None]
    n = np.arange(coarse, dtype=np.float64)[None, :]
    k = np.arange(1, coarse // 2, dtype=np.float64)[:, None, None]
    total = 1.0 + 2.0 * np.sum(np.cos(2.0 * np.pi * k * (m / fine - n / coarse)), axis=0)
    total = total + np.cos(np.pi * n) * np.cos(np.pi * m * coarse / fine)
    return total / coarse


def tables(coarse):
    odd = interp_table(coarse)[1::2]
    order = np.concatenate([np.arange(0, coarse, 2), np.arange(1, coarse, 2)])
    along_x = odd[order][:, order]
    quad = np.eye(4)
    rows = np.array(
        [4 * jj + 2 * p + xp for xp in range(2) for p in range(2) for jj in range(coarse // 4)]
    )
    cols = np.array([2 * y + yp for yp in range(2) for y in range(coarse)])
    row_pick = np.zeros((coarse, coarse))
    row_pick[np.arange(coarse), rows] = 1.0
    col_pick = np.zeros((2 * coarse, 2 * coarse))
    col_pick[cols, np.arange(2 * coarse)] = 1.0

    tile = 16
    turn = np.zeros((tile * tile, tile * tile))
    for r in range(tile):
        for jj in range(tile):
            turn[r * tile + jj, jj * tile + r] = 1.0

    def low(array):
        return jnp.asarray(np.ascontiguousarray(array), F32).astype(BF16)

    return {
        "ax": low(along_x),
        "axt": low(along_x.T),
        "yup": low(np.kron(quad, odd.T)),
        "ydown": low(np.kron(quad, odd)),
        "turn": low(turn),
        "row": low(row_pick),
        "rowt": low(row_pick.T),
        "col": low(col_pick),
        "colt": low(col_pick.T),
    }


def dot(a, b):
    return jnp.dot(a, b, preferred_element_type=F32)


def stacked(src, r0, lanes):
    tiles = [src[pl.ds(r0, 16), j * lanes : (j + 1) * lanes] for j in range(32)]
    return jnp.concatenate(
        [jnp.concatenate(tiles[:16], axis=0), jnp.concatenate(tiles[16:], axis=0)], axis=1
    )


def density_kernel(
    coarse, steps, slots, bd, func, resp, ax, yup, turn, fe, fo, part, rm, me, mo, acc
):
    step = pl.program_id(0)
    half = coarse // 2
    quarter = coarse // 4
    lanes = 2 * coarse
    left = lax.broadcasted_iota(jnp.int32, (half, lanes), 1) < coarse
    left_all = lax.broadcasted_iota(jnp.int32, (lanes, lanes), 1) < coarse

    @pl.when(step == 0)
    def _():
        acc[...] = jnp.zeros_like(acc)

    width = 512
    for c in range(0, coarse * coarse, width):
        rm[:, c : c + width] = dot(bd[...], resp[:, c : c + width]).astype(BF16)

    def pair(i, carry):
        r0 = pl.multiple_of(i * 16, 16)
        g0 = i * 4
        for src, even, odd, at in ((func, fe, fo, g0), (rm, me, mo, 0)):
            t_all = dot(turn[...], stacked(src, r0, lanes))
            for g in range(4):
                t = []
                for k in range(4 * g, 4 * g + 4):
                    piece = t_all[16 * k : 16 * k + 16]
                    t.append(jnp.concatenate([piece[:, :lanes], piece[:, lanes:]], axis=0))
                evens, odds = [], []
                for k in (0, 2):
                    evens.append(jnp.where(left, t[k], pltpu.roll(t[k + 1], coarse, 1)))
                    odds.append(jnp.where(left, pltpu.roll(t[k], coarse, 1), t[k + 1]))
                x = jnp.concatenate(
                    [jnp.concatenate(evens, axis=1), jnp.concatenate(odds, axis=1)], axis=0
                ).astype(BF16)
                up = dot(ax[...], x).astype(BF16)
                even[at + g, 0:coarse, :] = x
                even[at + g, coarse:lanes, :] = up
                both = jnp.concatenate([x, up], axis=0)
                odd[at + g, :, :] = dot(both, yup[...]).astype(BF16)
        for b in range(2):
            sums = []
            for left_src, right_src in ((fe, me), (fo, mo)):
                total = None
                for g in (2 * b, 2 * b + 1):
                    prod = (left_src[g0 + g] * right_src[g]).astype(F32)
                    prod = prod[:, :lanes] + prod[:, lanes:]
                    total = prod if total is None else total + prod
                sums.append(total + pltpu.roll(total, coarse, 1))
            d = jnp.where(left_all, sums[0], sums[1])
            at = (step * STEP_BOXES + 2 * i + b) * 2
            for q in range(2):
                slot = slots[at + q]
                for c in range(4):
                    acc[slot, c * quarter : (c + 1) * quarter, :] += d[
                        c * half + q * quarter : c * half + (q + 1) * quarter, :
                    ]
        return carry

    lax.fori_loop(0, STEP_BOXES // 2, pair, 0, unroll=8)

    @pl.when(step == steps - 1)
    def _():
        part[...] = acc[...].astype(BF16)


def exchange_kernel(
    sizes, shifts, own, part, kxc, row, rowt, col, colt, ve, vo, out, got, pot, back, s1, r1, s2, r2
):
    coarse = kxc.shape[0]
    me = [lax.axis_index(name) for name in ("gx", "gy", "gz")]

    def device(shift, sign):
        return tuple(
            lax.rem(me[a] + (sign * shift[a]) % sizes[a], sizes[a]) for a in range(3)
        )

    others = [k for k in range(len(shifts)) if k != own]
    barrier = pltpu.get_barrier_semaphore()
    for k in others:
        pl.semaphore_signal(
            barrier, inc=1, device_id=device(shifts[k], -1), device_id_type=MESH
        )
    pl.semaphore_wait(barrier, len(others))
    first, second = {}, {}
    for k in others:
        first[k] = pltpu.make_async_remote_copy(
            src_ref=part.at[k],
            dst_ref=got.at[k],
            send_sem=s1.at[k],
            recv_sem=r1.at[k],
            device_id=device(shifts[k], 1),
            device_id_type=MESH,
        )
        first[k].start()
    high = lax.Precision.HIGHEST
    by_col = jnp.dot(kxc[...], col[...].astype(F32), precision=high)
    scale = jnp.dot(row[...].astype(F32), by_col, precision=high)
    total = part[own].astype(F32)
    for k in others:
        first[k].wait_recv()
        total = total + got[k].astype(F32)
    value = (scale * total).astype(BF16)
    pot[...] = value
    for k in others:
        second[k] = pltpu.make_async_remote_copy(
            src_ref=pot,
            dst_ref=back.at[k],
            send_sem=s2.at[k],
            recv_sem=r2.at[k],
            device_id=device(shifts[k], -1),
            device_id_type=MESH,
        )
        second[k].start()
    by_col = dot(value, colt[...]).astype(BF16)
    out[...] = dot(rowt[...], by_col).astype(BF16)
    left = lax.broadcasted_iota(jnp.int32, value.shape, 1) < coarse

    def spread(k, block):
        block = block.astype(F32)
        turned = pltpu.roll(block, coarse, 1)
        ve[k] = jnp.where(left, block, turned).astype(BF16)
        vo[k] = jnp.where(left, turned, block).astype(BF16)

    spread(own, value)
    for k in others:
        second[k].wait_recv()
        spread(k, back[k])
    for k in others:
        first[k].wait_send()
        second[k].wait_send()


def apply_kernel(coarse, slots, fe, fo, ve, vo, axt, ydown, out, s):
    step = pl.program_id(0)
    half = coarse // 2
    quarter = coarse // 4
    lanes = 2 * coarse
    left = lax.broadcasted_iota(jnp.int32, (half, lanes), 1) < coarse

    def pair(i, carry):
        r0 = pl.multiple_of(i * 16, 16)
        g0 = i * 4
        for b in range(2):
            at = (step * STEP_BOXES + 2 * i + b) * 2
            pieces = []
            for v in (ve, vo):
                rows = []
                for c in range(4):
                    for q in range(2):
                        rows.append(v[slots[at + q], c * quarter : (c + 1) * quarter, :])
                plane = jnp.concatenate(rows, axis=0)
                pieces.append(jnp.concatenate([plane, plane], axis=1))
            for g in (2 * b, 2 * b + 1):
                we = fe[g0 + g] * pieces[0]
                wo = fo[g0 + g] * pieces[1]
                z = we.astype(F32) + dot(wo, ydown[...])
                down = dot(axt[...], z[coarse:].astype(BF16))
                res = (z[:coarse] + down) * 0.25
                for k in (0, 2):
                    e = res[:half, k * coarse : (k + 2) * coarse]
                    o = res[half:, k * coarse : (k + 2) * coarse]
                    base = (4 * g + k) * half
                    s[base : base + half, :] = jnp.where(left, e, pltpu.roll(o, coarse, 1))
                    s[base + half : base + 2 * half, :] = jnp.where(
                        left, pltpu.roll(e, coarse, 1), o
                    )
        for j in range(half):
            out[pl.ds(r0, 16), j * lanes : (j + 1) * lanes] = s[
                pl.ds(j, 16, stride=half), :
            ].astype(BF16)
        return carry

    lax.fori_loop(0, STEP_BOXES // 2, pair, 0, unroll=8)


def on_device(sizes, functions, responses, box_domain, pair_index, pair_weight, kernel_xc):
    boxes, funs, cells = functions.shape
    coarse = math.isqrt(cells)
    lanes = 2 * coarse
    size_x, size_y, size_z = sizes
    near = (min(4, size_x), min(2, size_y), min(3, size_z))
    shifts = [
        (kx - 2, ky - 1, kz - 1)
        for kx in range(near[0])
        for ky in range(near[1])
        for kz in range(near[2])
    ]
    own = [k for k, sh in enumerate(shifts) if all(d % n == 0 for d, n in zip(sh, sizes))][0]
    count = len(shifts)
    t = tables(coarse)

    domain = box_domain[:, 0]
    tx = domain // (size_y * size_z)
    ty = domain // size_z % size_y
    tz = domain % size_z
    kx = (tx[:, None] + jnp.arange(2, dtype=jnp.int32) - lax.axis_index("gx") + 2) % size_x
    ky = (ty - lax.axis_index("gy") + 1) % size_y
    kz = (tz - lax.axis_index("gz") + 1) % size_z
    slots = (kx * near[1] + ky[:, None]) * near[2] + kz[:, None]
    slots = jnp.clip(slots, 0, count - 1).astype(jnp.int32).reshape(-1)

    rows = STEP_BOXES * funs
    first, second = pair_index[0], pair_index[1]
    f_of = jnp.arange(funs, dtype=jnp.int32)
    lane = jnp.arange(rows, dtype=jnp.int32)
    weight_f = jnp.where(first[:, None, :] == f_of[None, :, None], pair_weight[:, None, :], 0.0)
    same = second[:, None, :, None] == (lane % funs)[None, None, None, :]
    mixed = jnp.sum(jnp.where(same, weight_f[..., None], 0.0), axis=2)
    here = (jnp.arange(boxes, dtype=jnp.int32) % STEP_BOXES)[:, None] == (lane // funs)[None, :]
    bd = jnp.where(here[:, None, :], mixed, 0.0).astype(BF16).reshape(boxes * funs, rows)

    steps = boxes // STEP_BOXES
    groups = STEP_BOXES * funs // 4

    def whole(shape):
        return pl.BlockSpec(shape, lambda i, *_: (0,) * len(shape))

    fe, fo, part = pl.pallas_call(
        functools.partial(density_kernel, coarse, steps),
        grid_spec=pltpu.PrefetchScalarGridSpec(
            num_scalar_prefetch=1,
            grid=(steps,),
            in_specs=[
                pl.BlockSpec((rows, rows), lambda i, *_: (i, 0)),
                pl.BlockSpec((rows, cells), lambda i, *_: (i, 0)),
                pl.BlockSpec((rows, cells), lambda i, *_: (i, 0)),
                whole((coarse, coarse)),
                whole((4 * coarse, 4 * coarse)),
                whole((256, 256)),
            ],
            out_specs=[
                pl.BlockSpec((groups, lanes, 4 * coarse), lambda i, *_: (i, 0, 0)),
                pl.BlockSpec((groups, lanes, 4 * coarse), lambda i, *_: (i, 0, 0)),
                whole((count, coarse, lanes)),
            ],
            scratch_shapes=[
                pltpu.VMEM((rows, cells), BF16),
                pltpu.VMEM((4, lanes, 4 * coarse), BF16),
                pltpu.VMEM((4, lanes, 4 * coarse), BF16),
                pltpu.VMEM((count, coarse, lanes), F32),
            ],
        ),
        out_shape=[
            jax.ShapeDtypeStruct((steps * groups, lanes, 4 * coarse), BF16),
            jax.ShapeDtypeStruct((steps * groups, lanes, 4 * coarse), BF16),
            jax.ShapeDtypeStruct((count, coarse, lanes), BF16),
        ],
        name="density",
    )(
        slots,
        bd,
        functions.reshape(boxes * funs, cells),
        responses.reshape(boxes * funs, cells),
        t["ax"],
        t["yup"],
        t["turn"],
    )

    vm = pl.BlockSpec(memory_space=pltpu.VMEM)
    block = (count, coarse, lanes)
    ve, vo, potential = pl.pallas_call(
        functools.partial(exchange_kernel, sizes, shifts, own),
        in_specs=[vm] * 6,
        out_specs=[vm] * 3,
        out_shape=[
            jax.ShapeDtypeStruct(block, BF16),
            jax.ShapeDtypeStruct(block, BF16),
            jax.ShapeDtypeStruct((coarse, lanes), BF16),
        ],
        scratch_shapes=[
            pltpu.VMEM(block, BF16),
            pltpu.VMEM((coarse, lanes), BF16),
            pltpu.VMEM(block, BF16),
        ]
        + [pltpu.SemaphoreType.DMA((count,))] * 4,
        compiler_params=pltpu.CompilerParams(collective_id=0, has_side_effects=True),
        name="exchange",
    )(part, kernel_xc.reshape(coarse, lanes), t["row"], t["rowt"], t["col"], t["colt"])

    applied = pl.pallas_call(
        functools.partial(apply_kernel, coarse),
        grid_spec=pltpu.PrefetchScalarGridSpec(
            num_scalar_prefetch=1,
            grid=(steps,),
            in_specs=[
                pl.BlockSpec((groups, lanes, 4 * coarse), lambda i, *_: (i, 0, 0)),
                pl.BlockSpec((groups, lanes, 4 * coarse), lambda i, *_: (i, 0, 0)),
                whole(block),
                whole(block),
                whole((coarse, coarse)),
                whole((4 * coarse, 4 * coarse)),
            ],
            out_specs=pl.BlockSpec((rows, cells), lambda i, *_: (i, 0)),
            scratch_shapes=[pltpu.VMEM((16 * coarse // 2, lanes), F32)],
        ),
        out_shape=jax.ShapeDtypeStruct((boxes * funs, cells), BF16),
        name="apply",
    )(slots, fe, fo, ve, vo, t["axt"], t["ydown"])
    return applied.reshape(boxes, funs, cells), potential.reshape(1, coarse * lanes)


def solution(mesh):
    sizes = tuple(mesh.shape[name] for name in ("gx", "gy", "gz"))
    over = ("gx", "gy", "gz")
    in_specs = (
        P(over, None, None),
        P(over, None, None),
        P(over, None),
        P(None, over, None),
        P(over, None),
        P(over, None),
    )
    out_specs = (P(over, None, None), P(over, None))
    return jax.shard_map(
        functools.partial(on_device, sizes),
        mesh=mesh,
        in_specs=in_specs,
        out_specs=out_specs,
        check_vma=False,
    )
```

```python
import functools
import math

import jax
import jax.numpy as jnp
import numpy as np
from jax import lax
from jax.experimental import pallas as pl
from jax.experimental.pallas import tpu as pltpu
from jax.sharding import PartitionSpec as P

MESH = pl.DeviceIdType.MESH
F32 = jnp.float32
BF16 = jnp.bfloat16
STEP_BOXES = 16


def interp_table(coarse):
    fine = 2 * coarse
    m = np.arange(fine, dtype=np.float64)[:, None]
    n = np.arange(coarse, dtype=np.float64)[None, :]
    k = np.arange(1, coarse // 2, dtype=np.float64)[:, None, None]
    total = 1.0 + 2.0 * np.sum(np.cos(2.0 * np.pi * k * (m / fine - n / coarse)), axis=0)
    total = total + np.cos(np.pi * n) * np.cos(np.pi * m * coarse / fine)
    return total / coarse


def tables(coarse):
    odd = interp_table(coarse)[1::2]
    order = np.concatenate([np.arange(0, coarse, 2), np.arange(1, coarse, 2)])
    along_x = odd[order][:, order]
    quad = np.eye(4)
    rows = np.array(
        [4 * jj + 2 * p + xp for xp in range(2) for p in range(2) for jj in range(coarse // 4)]
    )
    cols = np.array([2 * y + yp for yp in range(2) for y in range(coarse)])
    row_pick = np.zeros((coarse, coarse))
    row_pick[np.arange(coarse), rows] = 1.0
    col_pick = np.zeros((2 * coarse, 2 * coarse))
    col_pick[cols, np.arange(2 * coarse)] = 1.0

    tile = 16
    turn = np.zeros((tile * tile, tile * tile))
    for r in range(tile):
        for jj in range(tile):
            turn[r * tile + jj, jj * tile + r] = 1.0

    def low(array):
        return jnp.asarray(np.ascontiguousarray(array), F32).astype(BF16)

    return {
        "ax": low(along_x),
        "axt": low(along_x.T),
        "yup": low(np.kron(quad, odd.T)),
        "ydown": low(np.kron(quad, odd)),
        "turn": low(turn),
        "row": low(row_pick),
        "rowt": low(row_pick.T),
        "col": low(col_pick),
        "colt": low(col_pick.T),
    }


def dot(a, b):
    return jnp.dot(a, b, preferred_element_type=F32)


def stacked(src, r0, lanes):
    tiles = [src[pl.ds(r0, 16), j * lanes : (j + 1) * lanes] for j in range(32)]
    return jnp.concatenate(
        [jnp.concatenate(tiles[:16], axis=0), jnp.concatenate(tiles[16:], axis=0)], axis=1
    )


def density_kernel(
    coarse, steps, slots, bd, func, resp, ax, yup, turn, fe, fo, part, rm, me, mo, acc
):
    step = pl.program_id(0)
    half = coarse // 2
    quarter = coarse // 4
    lanes = 2 * coarse
    left = lax.broadcasted_iota(jnp.int32, (half, lanes), 1) < coarse
    left_all = lax.broadcasted_iota(jnp.int32, (lanes, lanes), 1) < coarse

    @pl.when(step == 0)
    def _():
        acc[...] = jnp.zeros_like(acc)

    width = 512
    for c in range(0, coarse * coarse, width):
        rm[:, c : c + width] = dot(bd[...], resp[:, c : c + width]).astype(BF16)

    def pair(i, carry):
        r0 = pl.multiple_of(i * 16, 16)
        g0 = i * 4
        for src, even, odd, at in ((func, fe, fo, g0), (rm, me, mo, 0)):
            t_all = dot(turn[...], stacked(src, r0, lanes))
            for g in range(4):
                t = []
                for k in range(4 * g, 4 * g + 4):
                    piece = t_all[16 * k : 16 * k + 16]
                    t.append(jnp.concatenate([piece[:, :lanes], piece[:, lanes:]], axis=0))
                evens, odds = [], []
                for k in (0, 2):
                    evens.append(jnp.where(left, t[k], pltpu.roll(t[k + 1], coarse, 1)))
                    odds.append(jnp.where(left, pltpu.roll(t[k], coarse, 1), t[k + 1]))
                x = jnp.concatenate(
                    [jnp.concatenate(evens, axis=1), jnp.concatenate(odds, axis=1)], axis=0
                ).astype(BF16)
                up = dot(ax[...], x).astype(BF16)
                even[at + g, 0:coarse, :] = x
                even[at + g, coarse:lanes, :] = up
                both = jnp.concatenate([x, up], axis=0)
                odd[at + g, :, :] = dot(both, yup[...]).astype(BF16)
        for b in range(2):
            sums = []
            for left_src, right_src in ((fe, me), (fo, mo)):
                total = None
                for g in (2 * b, 2 * b + 1):
                    prod = (left_src[g0 + g] * right_src[g]).astype(F32)
                    prod = prod[:, :lanes] + prod[:, lanes:]
                    total = prod if total is None else total + prod
                sums.append(total + pltpu.roll(total, coarse, 1))
            d = jnp.where(left_all, sums[0], sums[1])
            at = (step * STEP_BOXES + 2 * i + b) * 2
            for q in range(2):
                slot = slots[at + q]
                for c in range(4):
                    acc[slot, c * quarter : (c + 1) * quarter, :] += d[
                        c * half + q * quarter : c * half + (q + 1) * quarter, :
                    ]
        return carry

    lax.fori_loop(0, STEP_BOXES // 2, pair, 0, unroll=8)

    @pl.when(step == steps - 1)
    def _():
        part[...] = acc[...].astype(BF16)


def exchange_kernel(
    sizes, shifts, own, part, kxc, row, rowt, col, colt, ve, vo, out, got, pot, back, s1, r1, s2, r2
):
    coarse = kxc.shape[0]
    me = [lax.axis_index(name) for name in ("gx", "gy", "gz")]

    def device(shift, sign):
        return tuple(
            lax.rem(me[a] + (sign * shift[a]) % sizes[a], sizes[a]) for a in range(3)
        )

    others = [k for k in range(len(shifts)) if k != own]
    barrier = pltpu.get_barrier_semaphore()
    for k in others:
        pl.semaphore_signal(
            barrier, inc=1, device_id=device(shifts[k], -1), device_id_type=MESH
        )
    pl.semaphore_wait(barrier, len(others))
    first, second = {}, {}
    for k in others:
        first[k] = pltpu.make_async_remote_copy(
            src_ref=part.at[k],
            dst_ref=got.at[k],
            send_sem=s1.at[k],
            recv_sem=r1.at[k],
            device_id=device(shifts[k], 1),
            device_id_type=MESH,
        )
        first[k].start()
    high = lax.Precision.HIGHEST
    by_col = jnp.dot(kxc[...], col[...].astype(F32), precision=high)
    scale = jnp.dot(row[...].astype(F32), by_col, precision=high)
    total = part[own].astype(F32)
    for k in others:
        first[k].wait_recv()
        total = total + got[k].astype(F32)
    value = (scale * total).astype(BF16)
    pot[...] = value
    for k in others:
        second[k] = pltpu.make_async_remote_copy(
            src_ref=pot,
            dst_ref=back.at[k],
            send_sem=s2.at[k],
            recv_sem=r2.at[k],
            device_id=device(shifts[k], -1),
            device_id_type=MESH,
        )
        second[k].start()
    by_col = dot(value, colt[...]).astype(BF16)
    out[...] = dot(rowt[...], by_col).astype(BF16)
    left = lax.broadcasted_iota(jnp.int32, value.shape, 1) < coarse

    def spread(k, block):
        block = block.astype(F32) * 0.25
        turned = pltpu.roll(block, coarse, 1)
        ve[k] = jnp.where(left, block, turned).astype(BF16)
        vo[k] = jnp.where(left, turned, block).astype(BF16)

    spread(own, value)
    for k in others:
        second[k].wait_recv()
        spread(k, back[k])
    for k in others:
        first[k].wait_send()
        second[k].wait_send()


def apply_kernel(coarse, slots, fe, fo, ve, vo, axt, ydown, out, s):
    step = pl.program_id(0)
    half = coarse // 2
    quarter = coarse // 4
    lanes = 2 * coarse
    left = lax.broadcasted_iota(jnp.int32, (half, lanes), 1) < coarse

    def pair(i, carry):
        r0 = pl.multiple_of(i * 16, 16)
        g0 = i * 4
        for b in range(2):
            at = (step * STEP_BOXES + 2 * i + b) * 2
            pieces = []
            for v in (ve, vo):
                rows = []
                for c in range(4):
                    for q in range(2):
                        rows.append(v[slots[at + q], c * quarter : (c + 1) * quarter, :])
                plane = jnp.concatenate(rows, axis=0)
                pieces.append(jnp.concatenate([plane, plane], axis=1))
            for g in (2 * b, 2 * b + 1):
                we = fe[g0 + g] * pieces[0]
                wo = fo[g0 + g] * pieces[1]
                z = we.astype(F32) + dot(wo, ydown[...])
                down = dot(axt[...], z[coarse:].astype(BF16))
                res = z[:coarse] + down
                for k in (0, 2):
                    e = res[:half, k * coarse : (k + 2) * coarse]
                    o = res[half:, k * coarse : (k + 2) * coarse]
                    base = (4 * g + k) * half
                    s[base : base + half, :] = jnp.where(left, e, pltpu.roll(o, coarse, 1))
                    s[base + half : base + 2 * half, :] = jnp.where(
                        left, pltpu.roll(e, coarse, 1), o
                    )
        for j in range(half):
            out[pl.ds(r0, 16), j * lanes : (j + 1) * lanes] = s[
                pl.ds(j, 16, stride=half), :
            ].astype(BF16)
        return carry

    lax.fori_loop(0, STEP_BOXES // 2, pair, 0, unroll=8)


def on_device(sizes, functions, responses, box_domain, pair_index, pair_weight, kernel_xc):
    boxes, funs, cells = functions.shape
    coarse = math.isqrt(cells)
    lanes = 2 * coarse
    size_x, size_y, size_z = sizes
    near = (min(4, size_x), min(2, size_y), min(3, size_z))
    shifts = [
        (kx - 2, ky - 1, kz - 1)
        for kx in range(near[0])
        for ky in range(near[1])
        for kz in range(near[2])
    ]
    own = [k for k, sh in enumerate(shifts) if all(d % n == 0 for d, n in zip(sh, sizes))][0]
    count = len(shifts)
    t = tables(coarse)

    domain = box_domain[:, 0]
    tx = domain // (size_y * size_z)
    ty = domain // size_z % size_y
    tz = domain % size_z
    kx = (tx[:, None] + jnp.arange(2, dtype=jnp.int32) - lax.axis_index("gx") + 2) % size_x
    ky = (ty - lax.axis_index("gy") + 1) % size_y
    kz = (tz - lax.axis_index("gz") + 1) % size_z
    slots = (kx * near[1] + ky[:, None]) * near[2] + kz[:, None]
    slots = jnp.clip(slots, 0, count - 1).astype(jnp.int32).reshape(-1)

    rows = STEP_BOXES * funs
    first, second = pair_index[0], pair_index[1]
    f_of = jnp.arange(funs, dtype=jnp.int32)
    lane = jnp.arange(rows, dtype=jnp.int32)
    weight_f = jnp.where(first[:, None, :] == f_of[None, :, None], pair_weight[:, None, :], 0.0)
    same = second[:, None, :, None] == (lane % funs)[None, None, None, :]
    mixed = jnp.sum(jnp.where(same, weight_f[..., None], 0.0), axis=2)
    here = (jnp.arange(boxes, dtype=jnp.int32) % STEP_BOXES)[:, None] == (lane // funs)[None, :]
    bd = jnp.where(here[:, None, :], mixed, 0.0).astype(BF16).reshape(boxes * funs, rows)

    steps = boxes // STEP_BOXES
    groups = STEP_BOXES * funs // 4

    def whole(shape):
        return pl.BlockSpec(shape, lambda i, *_: (0,) * len(shape))

    fe, fo, part = pl.pallas_call(
        functools.partial(density_kernel, coarse, steps),
        grid_spec=pltpu.PrefetchScalarGridSpec(
            num_scalar_prefetch=1,
            grid=(steps,),
            in_specs=[
                pl.BlockSpec((rows, rows), lambda i, *_: (i, 0)),
                pl.BlockSpec((rows, cells), lambda i, *_: (i, 0)),
                pl.BlockSpec((rows, cells), lambda i, *_: (i, 0)),
                whole((coarse, coarse)),
                whole((4 * coarse, 4 * coarse)),
                whole((256, 256)),
            ],
            out_specs=[
                pl.BlockSpec((groups, lanes, 4 * coarse), lambda i, *_: (i, 0, 0)),
                pl.BlockSpec((groups, lanes, 4 * coarse), lambda i, *_: (i, 0, 0)),
                whole((count, coarse, lanes)),
            ],
            scratch_shapes=[
                pltpu.VMEM((rows, cells), BF16),
                pltpu.VMEM((4, lanes, 4 * coarse), BF16),
                pltpu.VMEM((4, lanes, 4 * coarse), BF16),
                pltpu.VMEM((count, coarse, lanes), F32),
            ],
        ),
        out_shape=[
            jax.ShapeDtypeStruct((steps * groups, lanes, 4 * coarse), BF16),
            jax.ShapeDtypeStruct((steps * groups, lanes, 4 * coarse), BF16),
            jax.ShapeDtypeStruct((count, coarse, lanes), BF16),
        ],
        name="density",
    )(
        slots,
        bd,
        functions.reshape(boxes * funs, cells),
        responses.reshape(boxes * funs, cells),
        t["ax"],
        t["yup"],
        t["turn"],
    )

    vm = pl.BlockSpec(memory_space=pltpu.VMEM)
    block = (count, coarse, lanes)
    ve, vo, potential = pl.pallas_call(
        functools.partial(exchange_kernel, sizes, shifts, own),
        in_specs=[vm] * 6,
        out_specs=[vm] * 3,
        out_shape=[
            jax.ShapeDtypeStruct(block, BF16),
            jax.ShapeDtypeStruct(block, BF16),
            jax.ShapeDtypeStruct((coarse, lanes), BF16),
        ],
        scratch_shapes=[
            pltpu.VMEM(block, BF16),
            pltpu.VMEM((coarse, lanes), BF16),
            pltpu.VMEM(block, BF16),
        ]
        + [pltpu.SemaphoreType.DMA((count,))] * 4,
        compiler_params=pltpu.CompilerParams(collective_id=0, has_side_effects=True),
        name="exchange",
    )(part, kernel_xc.reshape(coarse, lanes), t["row"], t["rowt"], t["col"], t["colt"])

    applied = pl.pallas_call(
        functools.partial(apply_kernel, coarse),
        grid_spec=pltpu.PrefetchScalarGridSpec(
            num_scalar_prefetch=1,
            grid=(steps,),
            in_specs=[
                pl.BlockSpec((groups, lanes, 4 * coarse), lambda i, *_: (i, 0, 0)),
                pl.BlockSpec((groups, lanes, 4 * coarse), lambda i, *_: (i, 0, 0)),
                whole(block),
                whole(block),
                whole((coarse, coarse)),
                whole((4 * coarse, 4 * coarse)),
            ],
            out_specs=pl.BlockSpec((rows, cells), lambda i, *_: (i, 0)),
            scratch_shapes=[pltpu.VMEM((16 * coarse // 2, lanes), F32)],
        ),
        out_shape=jax.ShapeDtypeStruct((boxes * funs, cells), BF16),
        name="apply",
    )(slots, fe, fo, ve, vo, t["axt"], t["ydown"])
    return applied.reshape(boxes, funs, cells), potential.reshape(1, coarse * lanes)


def solution(mesh):
    sizes = tuple(mesh.shape[name] for name in ("gx", "gy", "gz"))
    over = ("gx", "gy", "gz")
    in_specs = (
        P(over, None, None),
        P(over, None, None),
        P(over, None),
        P(None, over, None),
        P(over, None),
        P(over, None),
    )
    out_specs = (P(over, None, None), P(over, None))
    return jax.shard_map(
        functools.partial(on_device, sizes),
        mesh=mesh,
        in_specs=in_specs,
        out_specs=out_specs,
        check_vma=False,
    )
```
